32 devices in a mesh: groups: 2 (over x), ctx: 16 (over z, y, core).
Axes of the slice: x: 2, y: 2, z: 4, core: 2. Of those that a mesh axis runs over, the one named last changes fastest.
Arguments:
- src_cache: bfloat16 [1024, 2, 2, 16, 1024], P(('groups', 'ctx')), parts along dimension 0, may hold values from -6 to 6
- src_blocks: int32 [1024], P('groups'), parts along dimension 0, may hold values from 0 to 511, as said below
- dst_blocks: int32 [1024], P('groups'), parts along dimension 0, may hold values from 0 to 511, as said below
- ctx_lengths: int32 [8], P('groups'), parts along dimension 0, may hold values from 1024 to 2048, as said below
- queries: bfloat16 [5, 2, 8, 16384], P(None, None, 'groups'), parts along dimension 2, may hold values from -120 to 120
- new_keys: bfloat16 [5, 2, 8, 1024], P(None, None, 'groups'), parts along dimension 2, may hold values from -16 to 16
- new_values: bfloat16 [5, 2, 8, 1024], P(None, None, 'groups'), parts along dimension 2, may hold values from -6 to 6
Outputs:
- dst_cache: bfloat16 [1024, 2, 2, 16, 1024], P(('groups', 'ctx')), parts along dimension 0
- attn_out: float32 [5, 2, 1024, 128], P(None, None, ('groups', 'ctx')), parts along dimension 2
The draws below stay inside these ranges and needn't reach their ends.
There are 2 independent parts, one for each index of `groups`. The reference program is written for one: setup_inputs(seed, part) draws one part's arguments, and reference() takes and returns one part's arrays. A program takes and returns all parts, laid end to end along the dimension named above; each array names one. Nothing has to cross between parts.
Inputs may be any that keep to these rules, and one draw needn't show every extreme that they name: `src_blocks`: A permutation of the blocks; device k of ctx holds source slots k * 32 to (k + 1) * 32 - 1. `dst_blocks`: A permutation of the blocks; device k of ctx holds destination slots k * 32 to (k + 1) * 32 - 1. At most 2 blocks goes from the source slots of one device to the destination slots of one device, and some pair of devices has exactly 2. `ctx_lengths`: some request has exactly 2048 cached tokens.
All inputs are finite; a program needn't handle non-finite values.
Results may differ from the reference program's by a relative error of at most 0.001.
Values may be sent and summed in bfloat16 or wider, within the bound.
No kernel may reach another device: no remote copies, remote signals or barrier semaphores. Data moves between devices by JAX's collectives and lax.ppermute only.
A program may use at most 256 MiB of HBM per device.

```python
import jax
import jax.numpy as jnp
from jax import lax

KVH = 8
HD = 128
QPG = 16
LAYERS = 2
REQS = 4
STEPS = 4
BLK = 16
BLK_DEV = 32
NBLK = 512
CTXLEN = 2048
CAP = 2
QH = 128
KVW = 1024


def block_tables(key):
    base = jax.random.fold_in(key, 11)
    perm_key, shift_key, dest_key = jax.random.split(base, 3)
    device_count = NBLK // BLK_DEV
    src_blocks = jax.random.permutation(perm_key, NBLK).astype(jnp.int32)
    shuffled = jax.random.permutation(shift_key, device_count).astype(jnp.int32)
    place_of = jnp.zeros((device_count,), jnp.int32).at[shuffled].set(jnp.arange(device_count, dtype=jnp.int32))
    device_ids = jnp.arange(device_count, dtype=jnp.int32)
    scores = jnp.where(device_ids == device_count // 2, 0, jnp.where(device_ids == 1, 1, place_of + 2)).astype(jnp.int32)
    order = jnp.argsort(scores, stable=True).astype(jnp.int32)
    shifts = jnp.tile(order, CAP)[:BLK_DEV]
    arrange = jax.vmap(lambda sub_key: jax.random.permutation(sub_key, BLK_DEV))(jax.random.split(dest_key, device_count)).astype(jnp.int32)
    target_dev = jnp.arange(device_count, dtype=jnp.int32)[:, None]
    slot_pos = jnp.arange(BLK_DEV, dtype=jnp.int32)[None, :]
    source_slot = (target_dev - shifts[None, :]) % device_count * BLK_DEV + slot_pos
    dest_slot = target_dev * BLK_DEV + arrange
    dst_blocks = jnp.zeros((NBLK,), jnp.int32).at[dest_slot.reshape(-1)].set(src_blocks[source_slot].reshape(-1))
    return (src_blocks, dst_blocks)


def draw_src_blocks(key, part):
    return block_tables(key)[0]


def draw_dst_blocks(key, part):
    return block_tables(key)[1]


def draw_ctx_lengths(key, part):
    base = jax.random.fold_in(key, 23)
    len_key, pick_key = jax.random.split(base)
    lengths = jax.random.randint(len_key, (REQS,), CTXLEN // 2, CTXLEN + 1).astype(jnp.int32)
    chosen = jax.random.randint(pick_key, (), 0, REQS)
    return lengths.at[chosen].set(CTXLEN).astype(jnp.int32)


def draw_src_cache(key, part):
    cache = jnp.clip(jax.random.normal(jax.random.fold_in(key, 5), (NBLK, LAYERS, 2, BLK, KVW), jnp.float32), -6.0, 6.0)
    return cache.astype(jnp.bfloat16)


def draw_queries(key, part):
    shape = (STEPS + 1, LAYERS, REQS, KVH, QPG, HD)
    base = jnp.clip(jax.random.normal(jax.random.fold_in(key, 7), shape, jnp.float32), -6.0, 6.0)
    base = jnp.clip(base, -120.0, 120.0)
    return base.reshape(STEPS + 1, LAYERS, REQS, QH * HD).astype(jnp.bfloat16)


def noise(own_key, shape, width, reach, kind=jnp.bfloat16):
    return jnp.clip(width * jax.random.normal(own_key, shape, jnp.float32), -reach, reach).astype(kind)


def setup_inputs(seed: int = 0, part: int = 0) -> dict:
    seeds = jax.random.split(jax.random.key(seed), 8)
    own_keys = jax.random.split(jax.random.fold_in(seeds[7], part), 8)
    src_cache = draw_src_cache(jax.random.fold_in(jax.random.fold_in(seeds[7], part), 71), part)
    src_blocks = draw_src_blocks(jax.random.fold_in(jax.random.fold_in(seeds[7], part), 71), part)
    dst_blocks = draw_dst_blocks(jax.random.fold_in(jax.random.fold_in(seeds[7], part), 71), part)
    ctx_lengths = draw_ctx_lengths(jax.random.fold_in(jax.random.fold_in(seeds[7], part), 71), part)
    queries = draw_queries(jax.random.fold_in(jax.random.fold_in(seeds[7], part), 71), part)
    new_keys = noise(own_keys[5], (STEPS + 1, LAYERS, REQS, KVW), 4.0, 16.0)
    new_values = noise(own_keys[6], (STEPS + 1, LAYERS, REQS, KVW), 1.0, 6.0)
    return dict(src_cache=src_cache, src_blocks=src_blocks, dst_blocks=dst_blocks, ctx_lengths=ctx_lengths, queries=queries, new_keys=new_keys, new_values=new_values)


def reference(src_cache, src_blocks, dst_blocks, ctx_lengths, queries, new_keys, new_values):
    block_total = src_blocks.shape[0]
    slot_ids = jnp.arange(block_total, dtype=jnp.int32)
    inv_src = jnp.zeros((block_total,), jnp.int32).at[src_blocks].set(slot_ids)
    dst_cache = jnp.take(src_cache, inv_src[dst_blocks], axis=0)
    per_request = block_total // REQS
    ordered = jnp.take(src_cache, inv_src, axis=0)
    ordered = ordered.reshape(REQS, per_request, LAYERS, 2, BLK, KVH, HD)
    ordered = jnp.transpose(ordered, (2, 3, 0, 1, 4, 5, 6)).reshape(LAYERS, 2, REQS, CTXLEN, KVH, HD)
    positions = jnp.arange(CTXLEN, dtype=jnp.int32)
    in_context = positions[None, :] < ctx_lengths[:, None]
    score_scale = HD ** -0.5
    highest = lax.Precision.HIGHEST
    results = []
    for step_idx in range(STEPS + 1):
        per_layer = []
        for layer_idx in range(LAYERS):
            query_heads = queries[step_idx, layer_idx].reshape(REQS, KVH, QPG, HD).astype(jnp.float32)
            cache_keys = ordered[layer_idx, 0].astype(jnp.float32)
            cache_scores = jnp.einsum('rkgd,rtkd->rkgt', query_heads, cache_keys, precision=highest) * score_scale
            cache_scores = jnp.where(in_context[:, None, None, :], cache_scores, -jnp.inf)
            fresh_keys = new_keys[:step_idx + 1, layer_idx].reshape(step_idx + 1, REQS, KVH, HD).astype(jnp.float32)
            fresh_scores = jnp.einsum('rkgd,srkd->rkgs', query_heads, fresh_keys, precision=highest) * score_scale
            row_max = jnp.maximum(jnp.max(cache_scores, axis=-1), jnp.max(fresh_scores, axis=-1))
            cache_weights = jnp.exp(cache_scores - row_max[..., None])
            fresh_weights = jnp.exp(fresh_scores - row_max[..., None])
            totals = jnp.sum(cache_weights, axis=-1) + jnp.sum(fresh_weights, axis=-1)
            fresh_vals = new_values[:step_idx + 1, layer_idx].reshape(step_idx + 1, REQS, KVH, HD).astype(jnp.float32)
            weighted = jnp.einsum('rkgt,rtkd->rkgd', cache_weights, ordered[layer_idx, 1].astype(jnp.float32), precision=highest)
            weighted = weighted + jnp.einsum('rkgs,srkd->rkgd', fresh_weights, fresh_vals, precision=highest)
            per_layer.append((weighted / totals[..., None]).reshape(REQS * QH, HD))
        results.append(jnp.stack(per_layer))
    return dst_cache, jnp.stack(results)
```

```python
import functools

import jax
import jax.numpy as jnp
from jax import lax
from jax.experimental import pallas as pl
from jax.experimental.pallas import tpu as pltpu
from jax.sharding import PartitionSpec as P

KVH = 8
HD = 128
LOG2E = 1.4426950408889634
NEG = -1e30
STAT = 8


def move_body(count, idx_ref, src_ref, dst_ref, sems):
    copies = [
        pltpu.make_async_copy(src_ref.at[idx_ref[c]], dst_ref.at[c], sems.at[c])
        for c in range(count)
    ]
    for copy in copies:
        copy.start()
    for copy in copies:
        copy.wait()


def move_blocks(src, idx):
    count = idx.shape[0]
    return pl.pallas_call(
        functools.partial(move_body, count),
        out_shape=jax.ShapeDtypeStruct((count,) + src.shape[1:], src.dtype),
        grid_spec=pltpu.PrefetchScalarGridSpec(
            num_scalar_prefetch=1,
            grid=(1,),
            in_specs=[pl.BlockSpec(memory_space=pl.ANY)],
            out_specs=pl.BlockSpec(memory_space=pl.ANY),
            scratch_shapes=[pltpu.SemaphoreType.DMA((count,))],
        ),
        name="move_blocks",
    )(idx, src)


def eye_mask(rows):
    return lax.broadcasted_iota(jnp.int32, (rows, HD), 0) == lax.broadcasted_iota(
        jnp.int32, (rows, HD), 1
    )


def to_lanes(value, mask):
    return jnp.sum(jnp.where(mask, value, 0.0), axis=0, keepdims=True)


def to_column(lanes, mask):
    return jnp.sum(jnp.where(mask, lanes, 0.0), axis=1, keepdims=True)


def stat_tile(max_lanes, total_lanes):
    row = lax.broadcasted_iota(jnp.int32, (STAT, HD), 0)
    return jnp.where(row == 0, max_lanes, jnp.where(row == 1, total_lanes, 0.0))


def split_dot(weights, values):
    rows = weights.shape[0]
    high = weights.astype(jnp.bfloat16)
    low = (weights - high.astype(jnp.float32)).astype(jnp.bfloat16)
    both = jnp.dot(
        jnp.concatenate([high, low], axis=0), values, preferred_element_type=jnp.float32
    )
    return both[:rows] + both[rows:]


def partial_of(query, keys, values_ones, bias, scale):
    scores = lax.dot_general(
        query, keys, (((1,), (1,)), ((), ())), preferred_element_type=jnp.float32
    )
    scores = scores * scale + bias
    top = jnp.max(scores, axis=1, keepdims=True)
    both = split_dot(jnp.exp2(scores - top), values_ones)
    return top, both[:, :HD], both[:, HD:]


def with_ones(values):
    return jnp.concatenate([values, jnp.ones_like(values)], axis=1)


def attend_body(geo, bit_ref, q_ref, k_ref, v_ref, bias_ref, send_ref, keep_ref):
    requests, layers, pieces, flats, rows, scale = geo
    layer, head = pl.program_id(0), pl.program_id(1)
    tokens = k_ref.shape[0] * k_ref.shape[3]
    keys = k_ref[:, 0, 0].reshape(tokens, HD)
    values = with_ones(v_ref[:, 0, 0].reshape(tokens, HD))
    mask = eye_mask(rows)
    heads = pl.num_programs(1)
    for req in range(requests):
        query = q_ref[0, 0, req * pieces * rows:(req + 1) * pieces * rows]
        top, sums, totals = partial_of(query, keys, values, bias_ref[req:req + 1], scale)
        for piece in range(pieces):
            part = slice(piece * rows, (piece + 1) * rows)
            tile = stat_tile(to_lanes(top[part], mask), to_lanes(totals[part], mask))
            flat = (req * heads + head) * pieces + piece
            share = flat // flats
            chunk = (flat % flats) * layers + layer
            out_sums = sums[part]

            def put(ref):
                ref[share // 2, chunk, :rows, :] = out_sums
                ref[share // 2, chunk, rows:, :] = tile

            pl.when(share % 2 == bit_ref[0])(functools.partial(put, keep_ref))
            pl.when(share % 2 != bit_ref[0])(functools.partial(put, send_ref))


def merge(first, second, rows, mask):
    max_a, max_b = first[rows:rows + 1], second[rows:rows + 1]
    top = jnp.maximum(max_a, max_b)
    fac_a, fac_b = jnp.exp2(max_a - top), jnp.exp2(max_b - top)
    total = first[rows + 1:rows + 2] * fac_a + second[rows + 1:rows + 2] * fac_b
    sums = first[:rows] * to_column(fac_a, mask) + second[:rows] * to_column(fac_b, mask)
    return sums, top, total


def merge_body(rows, bit_ref, have_ref, came_ref, send_ref, keep_ref):
    mask = eye_mask(rows)
    half, chunks = send_ref.shape[0], send_ref.shape[1]

    for choice, out_ref in ((1 - bit_ref[0], send_ref), (bit_ref[0], keep_ref)):

        def step(i, carry, choice=choice, out_ref=out_ref):
            share, chunk = i // chunks, i % chunks
            where = 2 * share + choice
            sums, top, total = merge(have_ref[where, chunk], came_ref[where, chunk], rows, mask)
            out_ref[share, chunk, :rows, :] = sums
            out_ref[share, chunk, rows:, :] = stat_tile(top, total)
            return carry

        lax.fori_loop(0, half * chunks, step, 0)


def merge_halves(have, came, bit, rows):
    shape = jax.ShapeDtypeStruct((have.shape[0] // 2,) + have.shape[1:], have.dtype)
    full = pl.BlockSpec(have.shape, lambda i, b: (0, 0, 0, 0))
    part = pl.BlockSpec(shape.shape, lambda i, b: (0, 0, 0, 0))
    return pl.pallas_call(
        functools.partial(merge_body, rows),
        out_shape=(shape, shape),
        grid_spec=pltpu.PrefetchScalarGridSpec(
            num_scalar_prefetch=1, grid=(1,), in_specs=[full, full], out_specs=(part, part)
        ),
        name="merge_halves",
    )(bit, have, came)


def fresh_body(geo, q_ref, k_ref, v_ref, out_ref):
    rows, group, fresh, scale = geo
    mask = eye_mask(rows)
    chunks, width = k_ref.shape[0], k_ref.shape[1]
    step = lax.broadcasted_iota(jnp.int32, (rows, width), 0) // group
    token = lax.broadcasted_iota(jnp.int32, (rows, width), 1)
    bias = jnp.where((token <= step) & (token < fresh), 0.0, NEG)
    for chunk in range(chunks):
        top, sums, totals = partial_of(
            q_ref[chunk], k_ref[chunk], with_ones(v_ref[chunk]), bias, scale
        )
        out_ref[chunk, :rows, :] = sums
        out_ref[chunk, rows:, :] = stat_tile(to_lanes(top, mask), to_lanes(totals, mask))


def final_body(geo, have_ref, came_ref, fresh_ref, out_ref):
    rows, group, layers = geo
    mask = eye_mask(rows)
    for chunk in range(fresh_ref.shape[0]):
        sums, top, total = merge(have_ref[0, chunk], came_ref[0, chunk], rows, mask)
        both = jnp.concatenate([sums, stat_tile(top, total)], axis=0)
        sums, _, total = merge(both, fresh_ref[chunk], rows, mask)
        lane = lax.broadcasted_iota(jnp.int32, (1, HD), 1)
        total = jnp.where(lane < rows, total, 1.0)
        result = sums * to_column(1.0 / total, mask)
        flat, layer = chunk // layers, chunk % layers
        for step in range(rows // group):
            out_ref[step, layer, flat * group:(flat + 1) * group, :] = result[
                step * group:(step + 1) * group
            ]


def local(src_cache, src_blocks, dst_blocks, ctx_lengths, queries, new_keys, new_values):
    devices = lax.axis_size("ctx")
    me = lax.axis_index("ctx")
    per_dev, layers, _, block_len, _ = src_cache.shape
    block_total = src_blocks.shape[0]
    steps, _, requests, width = queries.shape
    group_all = width // (KVH * HD)
    per_request = block_total // requests
    capacity = (per_dev + devices - 1) // devices
    slot_ids = jnp.arange(block_total, dtype=jnp.int32)
    own_slots = jnp.arange(per_dev, dtype=jnp.int32)
    i32 = lambda flags: flags.astype(jnp.int32)

    own_src = lax.dynamic_slice_in_dim(src_blocks, me * per_dev, per_dev)
    own_dst = lax.dynamic_slice_in_dim(dst_blocks, me * per_dev, per_dev)
    goes_to = jnp.sum(i32(own_src[:, None] == dst_blocks[None, :]) * slot_ids[None, :], axis=1)
    target = goes_to // per_dev
    earlier = own_slots[None, :] < own_slots[:, None]
    rank = jnp.sum(i32((target[:, None] == target[None, :]) & earlier), axis=1)
    bucket = target * capacity + rank
    buckets = jnp.arange(devices * capacity, dtype=jnp.int32)
    chosen = jnp.sum(i32(buckets[:, None] == bucket[None, :]) * own_slots[None, :], axis=1)
    root = jnp.sum(i32(own_dst[:, None] == src_blocks[None, :]) * slot_ids[None, :], axis=1)
    origin = root // per_dev
    before = (origin[:, None] == origin[None, :]) & (root[None, :] < root[:, None])
    take_rows = origin * capacity + jnp.sum(i32(before), axis=1)

    outgoing = move_blocks(src_cache, chosen)
    arrived = lax.all_to_all(outgoing, "ctx", split_axis=0, concat_axis=0, tiled=True)

    pieces = max(1, devices // (requests * KVH))
    group = group_all // pieces
    flats = requests * KVH * pieces // devices
    rows = steps * group
    chunks = flats * layers
    scale = HD ** -0.5 * LOG2E
    query_rows = queries.reshape(steps, layers, requests, KVH, pieces, group, HD)
    query_rows = jnp.transpose(query_rows, (1, 3, 2, 4, 0, 5, 6))
    query_rows = query_rows.reshape(layers, KVH, requests * pieces * rows, HD)
    positions = (own_src % per_request)[:, None] * block_len + jnp.arange(
        block_len, dtype=jnp.int32
    )
    request_ids = jnp.arange(requests, dtype=jnp.int32)
    live = ((own_src // per_request)[None, :, None] == request_ids[:, None, None]) & (
        positions[None] < ctx_lengths[:, None, None]
    )
    bias = jnp.where(live, 0.0, NEG).astype(jnp.float32).reshape(requests, per_dev * block_len)
    bits = devices.bit_length() - 1
    bit_of = [((me >> b) & 1).astype(jnp.int32).reshape(1) for b in range(bits)]
    half = jax.ShapeDtypeStruct((devices // 2, chunks, rows + STAT, HD), jnp.float32)
    cache_block = (per_dev, 1, 1, block_len, HD)
    resident = pl.BlockSpec(half.shape, lambda l, k, b: (0, 0, 0, 0))
    send, keep = pl.pallas_call(
        functools.partial(attend_body, (requests, layers, pieces, flats, rows, scale)),
        out_shape=(half, half),
        grid_spec=pltpu.PrefetchScalarGridSpec(
            num_scalar_prefetch=1,
            grid=(layers, KVH),
            in_specs=[
                pl.BlockSpec((1, 1) + query_rows.shape[2:], lambda l, k, b: (l, k, 0, 0)),
                pl.BlockSpec(cache_block, lambda l, k, b: (0, l, 0, 0, k)),
                pl.BlockSpec(cache_block, lambda l, k, b: (0, l, 1, 0, k)),
                pl.BlockSpec(bias.shape, lambda l, k, b: (0, 0)),
            ],
            out_specs=(resident, resident),
        ),
        name="attend",
    )(bit_of[0], query_rows, src_cache, src_cache, bias)

    share = requests * KVH * group_all // devices
    heads = KVH * group_all
    own_req, own_head = me * share // heads, me * share % heads
    own_q = lax.dynamic_slice(
        queries, (0, 0, own_req, own_head * HD), (steps, layers, 1, share * HD)
    ).reshape(steps, layers, flats, group, HD)
    own_q = jnp.transpose(own_q, (2, 1, 0, 3, 4)).reshape(chunks, rows, HD)
    fresh_count = new_keys.shape[0]
    kv_heads = max(1, share // group_all)

    def own_fresh(tokens):
        own = lax.dynamic_slice(
            tokens,
            (0, 0, own_req, own_head // group_all * HD),
            (fresh_count, layers, 1, kv_heads * HD),
        ).reshape(fresh_count, layers, kv_heads, HD)
        own = jnp.repeat(jnp.transpose(own, (2, 1, 0, 3)), flats // kv_heads, axis=0)
        own = own.reshape(chunks, fresh_count, HD)
        return jnp.pad(own, ((0, 0), (0, -fresh_count % 16), (0, 0)))

    fresh = pl.pallas_call(
        functools.partial(fresh_body, (rows, group, fresh_count, scale)),
        out_shape=jax.ShapeDtypeStruct((chunks, rows + STAT, HD), jnp.float32),
        name="fresh",
    )(own_q, own_fresh(new_keys), own_fresh(new_values))

    for b in range(bits):
        pairs = [(i, i ^ (1 << b)) for i in range(devices)]
        came = lax.ppermute(send, "ctx", pairs)
        if b + 1 < bits:
            send, keep = merge_halves(keep, came, bit_of[b + 1], rows)
    attn_out = pl.pallas_call(
        functools.partial(final_body, (rows, group, layers)),
        out_shape=jax.ShapeDtypeStruct((steps, layers, share, HD), jnp.float32),
        name="final",
    )(keep, came, fresh)

    dst_cache = move_blocks(arrived, take_rows)
    return dst_cache, attn_out


def solution(mesh):
    in_specs = (
        P(("groups", "ctx"), None, None, None, None),
        P("groups"),
        P("groups"),
        P("groups"),
        P(None, None, "groups", None),
        P(None, None, "groups", None),
        P(None, None, "groups", None),
    )
    out_specs = (
        P(("groups", "ctx"), None, None, None, None),
        P(None, None, ("groups", "ctx"), None),
    )
    return jax.shard_map(local, mesh=mesh, in_specs=in_specs, out_specs=out_specs, check_vma=False)
```

```python
import functools

import jax
import jax.numpy as jnp
from jax import lax
from jax.experimental import pallas as pl
from jax.experimental.pallas import tpu as pltpu
from jax.sharding import PartitionSpec as P

KVH = 8
HD = 128
LOG2E = 1.4426950408889634
NEG = -1e30
STAT = 8


def move_body(count, idx_ref, src_ref, dst_ref, held, in_sems, out_sems):
    loads = [
        pltpu.make_async_copy(src_ref.at[idx_ref[c]], held.at[c], in_sems.at[c])
        for c in range(count)
    ]
    stores = [
        pltpu.make_async_copy(held.at[c], dst_ref.at[c], out_sems.at[c]) for c in range(count)
    ]
    for load in loads:
        load.start()
    for load, store in zip(loads, stores):
        load.wait()
        store.start()
    for store in stores:
        store.wait()


def move_blocks(src, idx):
    count = idx.shape[0]
    return pl.pallas_call(
        functools.partial(move_body, count),
        out_shape=jax.ShapeDtypeStruct((count,) + src.shape[1:], src.dtype),
        grid_spec=pltpu.PrefetchScalarGridSpec(
            num_scalar_prefetch=1,
            grid=(1,),
            in_specs=[pl.BlockSpec(memory_space=pl.ANY)],
            out_specs=pl.BlockSpec(memory_space=pl.ANY),
            scratch_shapes=[
                pltpu.VMEM((count,) + src.shape[1:], src.dtype),
                pltpu.SemaphoreType.DMA((count,)),
                pltpu.SemaphoreType.DMA((count,)),
            ],
        ),
        name="move_blocks",
    )(idx, src)


def eye_mask(rows):
    return lax.broadcasted_iota(jnp.int32, (rows, HD), 0) == lax.broadcasted_iota(
        jnp.int32, (rows, HD), 1
    )


def to_lanes(value, mask):
    return jnp.sum(jnp.where(mask, value, 0.0), axis=0, keepdims=True)


def to_column(lanes, mask):
    return jnp.sum(jnp.where(mask, lanes, 0.0), axis=1, keepdims=True)


def stat_tile(max_lanes, total_lanes):
    row = lax.broadcasted_iota(jnp.int32, (STAT, HD), 0)
    return jnp.where(row == 0, max_lanes, jnp.where(row == 1, total_lanes, 0.0))


def split_dot(weights, values):
    rows = weights.shape[0]
    high = weights.astype(jnp.bfloat16)
    low = (weights - high.astype(jnp.float32)).astype(jnp.bfloat16)
    both = jnp.dot(
        jnp.concatenate([high, low], axis=0), values, preferred_element_type=jnp.float32
    )
    return both[:rows] + both[rows:]


def partial_of(query, keys, values_ones, bias, scale):
    scores = lax.dot_general(
        query, keys, (((1,), (1,)), ((), ())), preferred_element_type=jnp.float32
    )
    scores = scores * scale + bias
    top = jnp.max(scores, axis=1, keepdims=True)
    both = split_dot(jnp.exp2(scores - top), values_ones)
    return top, both[:, :HD], both[:, HD:]


def with_ones(values):
    return jnp.concatenate([values, jnp.ones_like(values)], axis=1)


def attend_body(geo, bit_ref, q_ref, k_ref, v_ref, bias_ref, send_ref, keep_ref):
    requests, layers, pieces, flats, rows, scale = geo
    layer, head = pl.program_id(0), pl.program_id(1)
    tokens = k_ref.shape[0] * k_ref.shape[3]
    keys = k_ref[:, 0, 0].reshape(tokens, HD)
    values = with_ones(v_ref[:, 0, 0].reshape(tokens, HD))
    mask = eye_mask(rows)
    heads = pl.num_programs(1)
    for req in range(requests):
        query = q_ref[0, 0, req * pieces * rows:(req + 1) * pieces * rows]
        top, sums, totals = partial_of(query, keys, values, bias_ref[req:req + 1], scale)
        for piece in range(pieces):
            part = slice(piece * rows, (piece + 1) * rows)
            tile = stat_tile(to_lanes(top[part], mask), to_lanes(totals[part], mask))
            flat = (req * heads + head) * pieces + piece
            share = flat // flats
            chunk = (flat % flats) * layers + layer
            out_sums = sums[part]

            def put(ref):
                ref[share // 2, chunk, :rows, :] = out_sums
                ref[share // 2, chunk, rows:, :] = tile

            pl.when(share % 2 == bit_ref[0])(functools.partial(put, keep_ref))
            pl.when(share % 2 != bit_ref[0])(functools.partial(put, send_ref))


def merge(first, second, rows, mask):
    max_a, max_b = first[rows:rows + 1], second[rows:rows + 1]
    top = jnp.maximum(max_a, max_b)
    fac_a, fac_b = jnp.exp2(max_a - top), jnp.exp2(max_b - top)
    total = first[rows + 1:rows + 2] * fac_a + second[rows + 1:rows + 2] * fac_b
    sums = first[:rows] * to_column(fac_a, mask) + second[:rows] * to_column(fac_b, mask)
    return sums, top, total


def merge_body(rows, bit_ref, have_ref, came_ref, send_ref, keep_ref):
    mask = eye_mask(rows)
    half, chunks = send_ref.shape[0], send_ref.shape[1]

    for choice, out_ref in ((1 - bit_ref[0], send_ref), (bit_ref[0], keep_ref)):

        def step(i, carry, choice=choice, out_ref=out_ref):
            share, chunk = i // chunks, i % chunks
            where = 2 * share + choice
            sums, top, total = merge(have_ref[where, chunk], came_ref[where, chunk], rows, mask)
            out_ref[share, chunk, :rows, :] = sums
            out_ref[share, chunk, rows:, :] = stat_tile(top, total)
            return carry

        lax.fori_loop(0, half * chunks, step, 0)


def merge_halves(have, came, bit, rows):
    shape = jax.ShapeDtypeStruct((have.shape[0] // 2,) + have.shape[1:], have.dtype)
    full = pl.BlockSpec(have.shape, lambda i, b: (0, 0, 0, 0))
    part = pl.BlockSpec(shape.shape, lambda i, b: (0, 0, 0, 0))
    return pl.pallas_call(
        functools.partial(merge_body, rows),
        out_shape=(shape, shape),
        grid_spec=pltpu.PrefetchScalarGridSpec(
            num_scalar_prefetch=1, grid=(1,), in_specs=[full, full], out_specs=(part, part)
        ),
        name="merge_halves",
    )(bit, have, came)


def fresh_body(geo, q_ref, k_ref, v_ref, out_ref):
    rows, group, fresh, scale = geo
    mask = eye_mask(rows)
    chunks, width = k_ref.shape[0], k_ref.shape[1]
    step = lax.broadcasted_iota(jnp.int32, (rows, width), 0) // group
    token = lax.broadcasted_iota(jnp.int32, (rows, width), 1)
    bias = jnp.where((token <= step) & (token < fresh), 0.0, NEG)
    for chunk in range(chunks):
        top, sums, totals = partial_of(
            q_ref[chunk], k_ref[chunk], with_ones(v_ref[chunk]), bias, scale
        )
        out_ref[chunk, :rows, :] = sums
        out_ref[chunk, rows:, :] = stat_tile(to_lanes(top, mask), to_lanes(totals, mask))


def final_body(geo, have_ref, came_ref, fresh_ref, out_ref):
    rows, group, layers = geo
    mask = eye_mask(rows)
    for chunk in range(fresh_ref.shape[0]):
        sums, top, total = merge(have_ref[0, chunk], came_ref[0, chunk], rows, mask)
        both = jnp.concatenate([sums, stat_tile(top, total)], axis=0)
        sums, _, total = merge(both, fresh_ref[chunk], rows, mask)
        lane = lax.broadcasted_iota(jnp.int32, (1, HD), 1)
        total = jnp.where(lane < rows, total, 1.0)
        result = sums * to_column(1.0 / total, mask)
        flat, layer = chunk // layers, chunk % layers
        for step in range(rows // group):
            out_ref[step, layer, flat * group:(flat + 1) * group, :] = result[
                step * group:(step + 1) * group
            ]


def local(src_cache, src_blocks, dst_blocks, ctx_lengths, queries, new_keys, new_values):
    devices = lax.axis_size("ctx")
    me = lax.axis_index("ctx")
    per_dev, layers, _, block_len, _ = src_cache.shape
    block_total = src_blocks.shape[0]
    steps, _, requests, width = queries.shape
    group_all = width // (KVH * HD)
    per_request = block_total // requests
    capacity = (per_dev + devices - 1) // devices
    slot_ids = jnp.arange(block_total, dtype=jnp.int32)
    own_slots = jnp.arange(per_dev, dtype=jnp.int32)
    i32 = lambda flags: flags.astype(jnp.int32)

    own_src = lax.dynamic_slice_in_dim(src_blocks, me * per_dev, per_dev)
    own_dst = lax.dynamic_slice_in_dim(dst_blocks, me * per_dev, per_dev)
    goes_to = jnp.sum(i32(own_src[:, None] == dst_blocks[None, :]) * slot_ids[None, :], axis=1)
    target = goes_to // per_dev
    earlier = own_slots[None, :] < own_slots[:, None]
    rank = jnp.sum(i32((target[:, None] == target[None, :]) & earlier), axis=1)
    bucket = target * capacity + rank
    buckets = jnp.arange(devices * capacity, dtype=jnp.int32)
    chosen = jnp.sum(i32(buckets[:, None] == bucket[None, :]) * own_slots[None, :], axis=1)
    root = jnp.sum(i32(own_dst[:, None] == src_blocks[None, :]) * slot_ids[None, :], axis=1)
    origin = root // per_dev
    before = (origin[:, None] == origin[None, :]) & (root[None, :] < root[:, None])
    take_rows = origin * capacity + jnp.sum(i32(before), axis=1)

    outgoing = move_blocks(src_cache, chosen)
    arrived = lax.all_to_all(outgoing, "ctx", split_axis=0, concat_axis=0, tiled=True)

    pieces = max(1, devices // (requests * KVH))
    group = group_all // pieces
    flats = requests * KVH * pieces // devices
    rows = steps * group
    chunks = flats * layers
    scale = HD ** -0.5 * LOG2E
    query_rows = queries.reshape(steps, layers, requests, KVH, pieces, group, HD)
    query_rows = jnp.transpose(query_rows, (1, 3, 2, 4, 0, 5, 6))
    query_rows = query_rows.reshape(layers, KVH, requests * pieces * rows, HD)
    positions = (own_src % per_request)[:, None] * block_len + jnp.arange(
        block_len, dtype=jnp.int32
    )
    request_ids = jnp.arange(requests, dtype=jnp.int32)
    live = ((own_src // per_request)[None, :, None] == request_ids[:, None, None]) & (
        positions[None] < ctx_lengths[:, None, None]
    )
    bias = jnp.where(live, 0.0, NEG).astype(jnp.float32).reshape(requests, per_dev * block_len)
    bits = devices.bit_length() - 1
    bit_of = [((me >> b) & 1).astype(jnp.int32).reshape(1) for b in range(bits)]
    half = jax.ShapeDtypeStruct((devices // 2, chunks, rows + STAT, HD), jnp.float32)
    cache_block = (per_dev, 1, 1, block_len, HD)
    resident = pl.BlockSpec(half.shape, lambda l, k, b: (0, 0, 0, 0))
    send, keep = pl.pallas_call(
        functools.partial(attend_body, (requests, layers, pieces, flats, rows, scale)),
        out_shape=(half, half),
        grid_spec=pltpu.PrefetchScalarGridSpec(
            num_scalar_prefetch=1,
            grid=(layers, KVH),
            in_specs=[
                pl.BlockSpec((1, 1) + query_rows.shape[2:], lambda l, k, b: (l, k, 0, 0)),
                pl.BlockSpec(cache_block, lambda l, k, b: (0, l, 0, 0, k)),
                pl.BlockSpec(cache_block, lambda l, k, b: (0, l, 1, 0, k)),
                pl.BlockSpec(bias.shape, lambda l, k, b: (0, 0)),
            ],
            out_specs=(resident, resident),
        ),
        name="attend",
    )(bit_of[0], query_rows, src_cache, src_cache, bias)

    share = requests * KVH * group_all // devices
    heads = KVH * group_all
    own_req, own_head = me * share // heads, me * share % heads
    own_q = lax.dynamic_slice(
        queries, (0, 0, own_req, own_head * HD), (steps, layers, 1, share * HD)
    ).reshape(steps, layers, flats, group, HD)
    own_q = jnp.transpose(own_q, (2, 1, 0, 3, 4)).reshape(chunks, rows, HD)
    fresh_count = new_keys.shape[0]
    kv_heads = max(1, share // group_all)

    def own_fresh(tokens):
        own = lax.dynamic_slice(
            tokens,
            (0, 0, own_req, own_head // group_all * HD),
            (fresh_count, layers, 1, kv_heads * HD),
        ).reshape(fresh_count, layers, kv_heads, HD)
        own = jnp.repeat(jnp.transpose(own, (2, 1, 0, 3)), flats // kv_heads, axis=0)
        own = own.reshape(chunks, fresh_count, HD)
        return jnp.pad(own, ((0, 0), (0, -fresh_count % 16), (0, 0)))

    fresh = pl.pallas_call(
        functools.partial(fresh_body, (rows, group, fresh_count, scale)),
        out_shape=jax.ShapeDtypeStruct((chunks, rows + STAT, HD), jnp.float32),
        name="fresh",
    )(own_q, own_fresh(new_keys), own_fresh(new_values))

    for b in range(bits):
        pairs = [(i, i ^ (1 << b)) for i in range(devices)]
        came = lax.ppermute(send, "ctx", pairs)
        if b + 1 < bits:
            send, keep = merge_halves(keep, came, bit_of[b + 1], rows)
    attn_out = pl.pallas_call(
        functools.partial(final_body, (rows, group, layers)),
        out_shape=jax.ShapeDtypeStruct((steps, layers, share, HD), jnp.float32),
        name="final",
    )(keep, came, fresh)

    dst_cache = move_blocks(arrived, take_rows)
    return dst_cache, attn_out


def solution(mesh):
    in_specs = (
        P(("groups", "ctx"), None, None, None, None),
        P("groups"),
        P("groups"),
        P("groups"),
        P(None, None, "groups", None),
        P(None, None, "groups", None),
        P(None, None, "groups", None),
    )
    out_specs = (
        P(("groups", "ctx"), None, None, None, None),
        P(None, None, ("groups", "ctx"), None),
    )
    return jax.shard_map(local, mesh=mesh, in_specs=in_specs, out_specs=out_specs, check_vma=False)
```
